256 devices in a mesh: band: 4 (over z_hi, core), grid: 64 (over y, z_lo, x).
Axes of the slice: x: 4, y: 4, z: 8 (z_hi: 2, z_lo: 4; z = z_hi * 4 + z_lo), core: 2. Of those that a mesh axis runs over, the one named last changes fastest.
Arguments:
- orbitals: bfloat16 [256, 384, 32, 128], P('band', 'grid'), may hold values from -24 to 24, as said below
- potential: float32 [384, 32, 128], P('grid'), may hold values from -1 to 1
Outputs:
- gradient: float32 [256, 384, 32, 128], P('band', 'grid')
- intersection: float32 [256, 256], P('band')
- subspace: float32 [256, 256], P('band')
The draws below stay inside these ranges and needn't reach their ends.
Inputs may be any that keep to these rules, and one draw needn't show every extreme that they name: `orbitals`: orbital values of order one.
All inputs are finite; a program needn't handle non-finite values.
Results may differ from the reference program's by a relative error of at most 0.0003.
Values may be sent and summed in bfloat16 or wider, within the bound.
A program may use at most 128 MiB of HBM per device.

```python
import math
import jax
import jax.numpy as jnp
from jax import lax

ORBS = 256
NZ = 32
NY = 128
NX = 384


def draw_orbitals(key, part):
    key_field, key_orb, key_plane, key_common, key_coef = jax.random.split(key, 5)
    shape = (ORBS, NX, NZ, NY)
    orb_scale = jnp.exp(jax.random.uniform(key_orb, (ORBS, 1, 1, 1), jnp.float32, math.log(0.5), math.log(2.0)))
    plane_scale = jnp.exp(jax.random.uniform(key_plane, (1, NX, 1, 1), jnp.float32, math.log(0.5), math.log(2.0)))
    base = jax.random.normal(key_field, shape, jnp.float32)
    common = jax.random.normal(key_common, (1, NX, NZ, NY), jnp.float32)
    coef = jax.random.uniform(key_coef, (ORBS, 1, 1, 1), jnp.float32, -0.6, 0.6)
    field = jnp.clip(base + coef * common, -6.0, 6.0)
    return (field * orb_scale * plane_scale).astype(jnp.bfloat16)


def block_levels(key, extent, cuts, smallest, top_value):
    factor_of = 1.0
    for position, parts in cuts:
        steps = jax.random.uniform(jax.random.fold_in(jax.random.fold_in(key, 6), position), (parts,), jnp.float32, smallest / len(cuts), top_value / len(cuts))
        factor_of = factor_of * jnp.repeat(jnp.exp(steps), extent[position] // parts).reshape((-1,) + (1,) * (len(extent) - 1 - position))
    return factor_of


def setup_inputs(seed: int = 0) -> dict:
    arg_keys = jax.random.split(jax.random.key(seed), 3)
    return {
        "orbitals": draw_orbitals(jax.random.fold_in(arg_keys[2], 71), 0),
        "potential": jnp.clip(jax.random.uniform(arg_keys[1], (NX, NZ, NY), jnp.float32, -1.0, 1.0) * block_levels(arg_keys[1], (NX, NZ, NY), ((0, 64),), -0.4, 0.0), -1.0, 1.0),
    }


COEFFS = (-49.0 / 18.0, 3.0 / 2.0, -3.0 / 20.0, 1.0 / 90.0)


def apply_hamiltonian(padded, potential):
    stencil_reach = len(COEFFS) - 1
    width_x = padded.shape[1] - 2 * stencil_reach
    planes = padded.shape[2]
    center = padded[:, stencil_reach:stencil_reach + width_x].astype(jnp.float32)
    z_padded = jnp.pad(center, ((0, 0), (0, 0), (stencil_reach, stencil_reach), (0, 0)))
    total = 3.0 * COEFFS[0] * center
    for shift_by in range(1, stencil_reach + 1):
        pair_x = padded[:, stencil_reach + shift_by:stencil_reach + shift_by + width_x].astype(jnp.float32) + padded[:, stencil_reach - shift_by:stencil_reach - shift_by + width_x].astype(jnp.float32)
        pair_z = z_padded[:, :, stencil_reach + shift_by:stencil_reach + shift_by + planes] + z_padded[:, :, stencil_reach - shift_by:stencil_reach - shift_by + planes]
        pair_y = jnp.roll(center, shift_by, 3) + jnp.roll(center, -shift_by, 3)
        total = total + COEFFS[shift_by] * (pair_x + pair_z + pair_y)
    return -0.5 * total + potential * center


def hamiltonian_group(group, potential):
    stencil_reach = len(COEFFS) - 1
    padded = jnp.pad(group, ((0, 0), (stencil_reach, stencil_reach), (0, 0), (0, 0)), mode="wrap")
    return apply_hamiltonian(padded, potential)


def reference(orbitals, potential):
    shape = orbitals.shape
    group_count = shape[0] // 16
    groups = orbitals.reshape((group_count, 16) + shape[1:])
    hpsi_half = lax.map(lambda group: hamiltonian_group(group, potential).astype(jnp.bfloat16), groups).reshape(shape)
    flat_psi = orbitals.reshape(shape[0], -1)
    flat_h = hpsi_half.reshape(shape[0], -1)
    cell_count = flat_psi.shape[1]
    intersection = jnp.dot(flat_psi, flat_psi.T, preferred_element_type=jnp.float32) / cell_count
    subspace = jnp.dot(flat_h, flat_psi.T, preferred_element_type=jnp.float32) / cell_count
    rayleigh = jnp.diagonal(subspace) / (jnp.diagonal(intersection) + 1e-6)

    def precondition(items):
        psi_group, ray_group = items
        h_group = hamiltonian_group(psi_group, potential)
        return (h_group - ray_group[:, None, None, None] * psi_group.astype(jnp.float32)) / (2.0 + potential)

    gradient = lax.map(precondition, (groups, rayleigh.reshape(group_count, 16))).reshape(shape)
    return gradient, intersection, subspace
```

```python
import functools
import jax
import jax.numpy as jnp
from jax import lax
from jax.experimental import pallas as pl
from jax.experimental.pallas import tpu as pltpu
from jax.sharding import PartitionSpec as P

COEFFS = (-49.0 / 18.0, 3.0 / 2.0, -3.0 / 20.0, 1.0 / 90.0)
MESH = pl.DeviceIdType.MESH


def padded_2(cells, sides, width):
    for axis, dim in sides:
        count = lax.axis_size(axis)
        head = lax.slice_in_dim(cells, 0, width, axis=dim)
        tail = lax.slice_in_dim(cells, cells.shape[dim] - width, cells.shape[dim], axis=dim)
        cells = jnp.concatenate(
            [
                lax.ppermute(tail, axis, [(i, (i + 1) % count) for i in range(count)]),
                cells,
                lax.ppermute(head, axis, [((i + 1) % count, i) for i in range(count)]),
            ],
            axis=dim,
        )
    return cells


def apply_hamiltonian(padded, potential):
    stencil_reach = len(COEFFS) - 1
    width_x = padded.shape[1] - 2 * stencil_reach
    planes = padded.shape[2]
    center = padded[:, stencil_reach : stencil_reach + width_x].astype(jnp.float32)
    z_padded = jnp.pad(center, ((0, 0), (0, 0), (stencil_reach, stencil_reach), (0, 0)))
    total = 3.0 * COEFFS[0] * center
    for shift_by in range(1, stencil_reach + 1):
        pair_x = padded[:, stencil_reach + shift_by : stencil_reach + shift_by + width_x].astype(
            jnp.float32
        ) + padded[:, stencil_reach - shift_by : stencil_reach - shift_by + width_x].astype(
            jnp.float32
        )
        pair_z = (
            z_padded[:, :, stencil_reach + shift_by : stencil_reach + shift_by + planes]
            + z_padded[:, :, stencil_reach - shift_by : stencil_reach - shift_by + planes]
        )
        pair_y = jnp.roll(center, shift_by, 3) + jnp.roll(center, -shift_by, 3)
        total = total + COEFFS[shift_by] * (pair_x + pair_z + pair_y)
    return -0.5 * total + potential * center


def row_products(left, right):
    return lax.dot_general(
        left, right, (((1,), (1,)), ((), ())), preferred_element_type=jnp.float32
    )


STRIDES = (1, 16, 4)
SIDE = 4


def grid_sum_kernel(v_ref, o_ref, bx, by, bz, qx, gy, gx, send_sem, recv_sem):
    me = lax.axis_index("grid")
    band = lax.axis_index("band")
    rows = v_ref.shape[0]
    rows_x, rows_y = rows // SIDE, rows // SIDE // SIDE
    coord = [lax.rem(lax.div(me, s), SIDE) for s in STRIDES]

    def peer(axis, d):
        other = lax.rem(coord[axis] + d, SIDE)
        return other, (band, me + (other - coord[axis]) * STRIDES[axis])

    barrier = pltpu.get_barrier_semaphore()
    for axis in range(3):
        for d in range(1, SIDE):
            pl.semaphore_signal(barrier, inc=1, device_id=peer(axis, d)[1], device_id_type=MESH)
    pl.semaphore_wait(barrier, 3 * (SIDE - 1))

    def exchange(phase, axis, source, landing):
        mine = coord[axis]
        copies = []
        for d in range(1, SIDE):
            other, device = peer(axis, d)
            copy = pltpu.make_async_remote_copy(
                src_ref=source(other),
                dst_ref=landing(mine),
                send_sem=send_sem.at[phase, d],
                recv_sem=recv_sem.at[phase, d],
                device_id=device,
                device_id_type=MESH,
            )
            copy.start()
            copies.append(copy)
        return copies

    def finish(copies):
        for copy in copies:
            copy.wait()

    def piece(ref, n):
        return lambda c: ref.at[pl.ds(pl.multiple_of(c * n, n), n)]

    copies = exchange(0, 0, piece(v_ref, rows_x), lambda c: bx.at[c])
    bx[coord[0]] = v_ref[pl.ds(pl.multiple_of(coord[0] * rows_x, rows_x), rows_x)]
    finish(copies)
    qx[...] = (bx[0] + bx[1]) + (bx[2] + bx[3])

    copies = exchange(1, 1, piece(qx, rows_y), lambda c: by.at[c])
    by[coord[1]] = qx[pl.ds(pl.multiple_of(coord[1] * rows_y, rows_y), rows_y)]
    finish(copies)
    bz[coord[2]] = (by[0] + by[1]) + (by[2] + by[3])

    copies = exchange(2, 2, lambda c: bz.at[coord[2]], lambda c: bz.at[c])
    finish(copies)
    gy[coord[1]] = (bz[0] + bz[1]) + (bz[2] + bz[3])

    copies = exchange(3, 1, lambda c: gy.at[coord[1]], lambda c: gy.at[c])
    finish(copies)
    gx[coord[0]] = gy[...].reshape(rows_x, gy.shape[-1])

    copies = exchange(4, 0, lambda c: gx.at[coord[0]], lambda c: gx.at[c])
    finish(copies)
    o_ref[...] = gx[...].reshape(o_ref.shape)


def grid_sum(v, collective_id):
    rows, cols = v.shape
    rows_x, rows_y = rows // SIDE, rows // SIDE // SIDE
    f32 = jnp.float32
    return pl.pallas_call(
        grid_sum_kernel,
        out_shape=jax.ShapeDtypeStruct(v.shape, f32),
        in_specs=[pl.BlockSpec(memory_space=pltpu.VMEM)],
        out_specs=pl.BlockSpec(memory_space=pltpu.VMEM),
        scratch_shapes=[
            pltpu.VMEM((SIDE, rows_x, cols), f32),
            pltpu.VMEM((SIDE, rows_y, cols), f32),
            pltpu.VMEM((SIDE, rows_y, cols), f32),
            pltpu.VMEM((rows_x, cols), f32),
            pltpu.VMEM((SIDE, rows_y, cols), f32),
            pltpu.VMEM((SIDE, rows_x, cols), f32),
            pltpu.SemaphoreType.DMA((5, SIDE)),
            pltpu.SemaphoreType.DMA((5, SIDE)),
        ],
        compiler_params=pltpu.CompilerParams(
            collective_id=collective_id, has_side_effects=True, vmem_limit_bytes=4 << 20
        ),
        name="grid_sum",
    )(v)


def body(orbitals, potential):
    shape = orbitals.shape
    orb_dev = shape[0]
    cell_count = shape[1] * lax.axis_size("grid") * shape[2] * shape[3]
    group_count = orb_dev // 16
    stencil_reach = len(COEFFS) - 1
    padded = padded_2(orbitals, (("grid", 1),), stencil_reach)
    groups = padded.reshape((group_count, 16) + padded.shape[1:])
    hpsi = lax.map(lambda group: apply_hamiltonian(group, potential), groups).reshape(shape)
    flat_psi = orbitals.reshape(orb_dev, -1)
    flat_h = hpsi.astype(jnp.bfloat16).reshape(orb_dev, -1)
    panel_rows = lax.all_gather(flat_psi, "band", axis=0, tiled=True)
    s_rows = row_products(flat_psi, panel_rows)
    h_rows = row_products(flat_h, panel_rows)
    columns = s_rows.shape[1]
    summed = grid_sum(jnp.concatenate([s_rows, h_rows], 0).reshape(-1, 128), 1)
    summed = summed.reshape(2 * orb_dev, columns)
    s_summed, h_summed = summed[:orb_dev], summed[orb_dev:]
    intersection = s_summed / cell_count
    subspace = h_summed / cell_count
    offset_rows = lax.axis_index("band") * orb_dev
    s_diag = jnp.diagonal(lax.dynamic_slice_in_dim(intersection, offset_rows, orb_dev, 1))
    h_diag = jnp.diagonal(lax.dynamic_slice_in_dim(subspace, offset_rows, orb_dev, 1))
    rayleigh = h_diag / (s_diag + 1e-06)
    gradient = (hpsi - rayleigh[:, None, None, None] * orbitals.astype(jnp.float32)) / (
        2.0 + potential
    )
    return (gradient, intersection, subspace)


def solution(mesh):
    in_specs = (P("band", "grid", None, None), P("grid", None, None))
    out_specs = (P("band", "grid", None, None), P("band", None), P("band", None))
    return jax.shard_map(body, mesh=mesh, in_specs=in_specs, out_specs=out_specs, check_vma=False)
```

```python
import jax
import jax.numpy as jnp
from jax import lax
from jax.experimental import pallas as pl
from jax.experimental.pallas import tpu as pltpu
from jax.sharding import PartitionSpec as P

COEFFS = (-49.0 / 18.0, 3.0 / 2.0, -3.0 / 20.0, 1.0 / 90.0)
HALVED = tuple(-0.5 * c for c in COEFFS)
REACH = len(COEFFS) - 1
MESH = pl.DeviceIdType.MESH
F32 = jnp.float32
BF16 = jnp.bfloat16

CUT = 18
WINDOW = 18


def upper_chip():
    return lax.div(lax.axis_index("band"), 2)


STRIDES = (1, 16, 4)
SIDE = 4


def grid_sum_kernel(v_ref, o_ref, bx, by, bz, qx, gy, gx, send_sem, recv_sem):
    me = lax.axis_index("grid")
    band = lax.axis_index("band")
    rows = v_ref.shape[0]
    rows_x, rows_y = rows // SIDE, rows // SIDE // SIDE
    coord = [lax.rem(lax.div(me, s), SIDE) for s in STRIDES]

    def peer(axis, d):
        other = lax.rem(coord[axis] + d, SIDE)
        return other, (band, me + (other - coord[axis]) * STRIDES[axis])

    barrier = pltpu.get_barrier_semaphore()
    for axis in range(3):
        for d in range(1, SIDE):
            pl.semaphore_signal(barrier, inc=1, device_id=peer(axis, d)[1], device_id_type=MESH)
    pl.semaphore_wait(barrier, 3 * (SIDE - 1))

    def exchange(phase, axis, source, landing):
        mine = coord[axis]
        copies = []
        for d in range(1, SIDE):
            other, device = peer(axis, d)
            copy = pltpu.make_async_remote_copy(
                src_ref=source(other),
                dst_ref=landing(mine),
                send_sem=send_sem.at[phase, d],
                recv_sem=recv_sem.at[phase, d],
                device_id=device,
                device_id_type=MESH,
            )
            copy.start()
            copies.append(copy)
        return copies

    def finish(copies):
        for copy in copies:
            copy.wait()

    def piece(ref, n):
        return lambda c: ref.at[pl.ds(pl.multiple_of(c * n, n), n)]

    copies = exchange(0, 0, piece(v_ref, rows_x), lambda c: bx.at[c])
    bx[coord[0]] = v_ref[pl.ds(pl.multiple_of(coord[0] * rows_x, rows_x), rows_x)]
    finish(copies)
    qx[...] = (bx[0] + bx[1]) + (bx[2] + bx[3])

    copies = exchange(1, 1, piece(qx, rows_y), lambda c: by.at[c])
    by[coord[1]] = qx[pl.ds(pl.multiple_of(coord[1] * rows_y, rows_y), rows_y)]
    finish(copies)
    bz[coord[2]] = (by[0] + by[1]) + (by[2] + by[3])

    copies = exchange(2, 2, lambda c: bz.at[coord[2]], lambda c: bz.at[c])
    finish(copies)
    gy[coord[1]] = (bz[0] + bz[1]) + (bz[2] + bz[3])

    copies = exchange(3, 1, lambda c: gy.at[coord[1]], lambda c: gy.at[c])
    finish(copies)
    gx[coord[0]] = gy[...].reshape(rows_x, gy.shape[-1])

    copies = exchange(4, 0, lambda c: gx.at[coord[0]], lambda c: gx.at[c])
    finish(copies)
    o_ref[...] = gx[...].reshape(o_ref.shape)


def grid_sum(v, collective_id):
    rows, cols = v.shape
    rows_x, rows_y = rows // SIDE, rows // SIDE // SIDE
    return pl.pallas_call(
        grid_sum_kernel,
        out_shape=jax.ShapeDtypeStruct(v.shape, F32),
        in_specs=[pl.BlockSpec(memory_space=pltpu.VMEM)],
        out_specs=pl.BlockSpec(memory_space=pltpu.VMEM),
        scratch_shapes=[
            pltpu.VMEM((SIDE, rows_x, cols), F32),
            pltpu.VMEM((SIDE, rows_y, cols), F32),
            pltpu.VMEM((SIDE, rows_y, cols), F32),
            pltpu.VMEM((rows_x, cols), F32),
            pltpu.VMEM((SIDE, rows_y, cols), F32),
            pltpu.VMEM((SIDE, rows_x, cols), F32),
            pltpu.SemaphoreType.DMA((5, SIDE)),
            pltpu.SemaphoreType.DMA((5, SIDE)),
        ],
        compiler_params=pltpu.CompilerParams(
            collective_id=collective_id, has_side_effects=True, vmem_limit_bytes=4 << 20
        ),
        name="grid_sum",
    )(v)


def stencil_kernel(psi_ref, lo_ref, hi_ref, v_ref, hpsi_ref, half_ref, g_ref, field):
    layers, planes = psi_ref.shape[:2]

    @pl.when(pl.program_id(0) == 0)
    def _():
        edge = jnp.zeros((layers + 2 * REACH, REACH) + psi_ref.shape[2:], F32)
        field[:, :REACH] = edge
        field[:, REACH + planes :] = edge

    @pl.loop(0, planes)
    def _(z):
        for x in range(REACH):
            field[x, z + REACH] = lo_ref[x, z].astype(F32)
            field[x + REACH + layers, z + REACH] = hi_ref[x, z].astype(F32)
        for x in range(layers):
            field[x + REACH, z + REACH] = psi_ref[x, z].astype(F32)

    @pl.loop(0, planes)
    def _(z):
        for x in range(layers):
            i, j = x + REACH, z + REACH
            center = field[i, j]
            total = (3.0 * HALVED[0] + v_ref[x, pl.ds(z, 1), :]) * center
            for k in range(1, REACH + 1):
                pair_x = field[i + k, j] + field[i - k, j]
                pair_z = field[i, j + k] + field[i, j - k]
                pair_y = pltpu.roll(center, k, 1) + pltpu.roll(center, center.shape[1] - k, 1)
                total = total + HALVED[k] * (pair_x + pair_z + pair_y)
            hpsi_ref[x, z] = total
            half_ref[x, z] = total.astype(BF16)

    upper = upper_chip()
    first = upper * (planes - WINDOW)
    for x in range(layers):
        for i in range(WINDOW):
            g_ref[x, i] = half_ref[x, first + i]

    @pl.when(upper == 1)
    def _():
        for x in range(layers):
            for z in range(planes - WINDOW, CUT + REACH):
                if z < CUT:
                    total = jnp.zeros(psi_ref.shape[2:], F32)
                    for k in range(CUT - z, REACH + 1):
                        total = total + HALVED[k] * field[x + REACH, z + REACH + k]
                else:
                    total = hpsi_ref[x, z]
                    for k in range(z - CUT + 1, REACH + 1):
                        total = total - HALVED[k] * field[x + REACH, z + REACH - k]
                g_ref[x, z - (planes - WINDOW)] = total.astype(BF16)


def stencil(psi, lo, hi, potential):
    layers, planes, orbs, ny = psi.shape
    block = 16

    def spec(n, m):
        return pl.BlockSpec((n, m, block, ny), lambda o: (0, 0, o, 0))

    return pl.pallas_call(
        stencil_kernel,
        grid=(orbs // block,),
        out_shape=(
            jax.ShapeDtypeStruct(psi.shape, F32),
            jax.ShapeDtypeStruct(psi.shape, BF16),
            jax.ShapeDtypeStruct((layers, WINDOW, orbs, ny), BF16),
        ),
        in_specs=[
            spec(layers, planes),
            spec(REACH, planes),
            spec(REACH, planes),
            pl.BlockSpec(potential.shape, lambda o: (0, 0, 0)),
        ],
        out_specs=(spec(layers, planes), spec(layers, planes), spec(layers, WINDOW)),
        scratch_shapes=[pltpu.VMEM((layers + 2 * REACH, planes + 2 * REACH, block, ny), F32)],
        compiler_params=pltpu.CompilerParams(vmem_limit_bytes=40 << 20),
        cost_estimate=pl.CostEstimate(flops=int(4e9), bytes_accessed=int(30e6), transcendentals=0),
        name="stencil",
    )(psi, lo, hi, potential)


def contract(left, right):
    return lax.dot_general(left, right, (((1,), (1,)), ((), ())), preferred_element_type=F32)


def chip_kernel(psi_ref, half_ref, par_ref, o_ref):
    @pl.when(pl.program_id(0) == 0)
    def _():
        o_ref[...] = jnp.zeros_like(o_ref)

    planes = psi_ref.shape[1]
    group = 8
    for z in range(0, planes, group):
        def wide(ref):
            return jnp.concatenate([ref[0, z + i] for i in range(group)], axis=1)

        psi = wide(psi_ref)
        left = jnp.concatenate([psi, wide(half_ref)], axis=0)
        right = jnp.concatenate([psi, wide(par_ref)], axis=0)
        o_ref[...] += contract(left, right)


def chip_products(psi, half, par):
    layers, planes, orbs, ny = psi.shape
    spec = pl.BlockSpec((1, planes, orbs, ny), lambda x: (x, 0, 0, 0))
    return pl.pallas_call(
        chip_kernel,
        grid=(layers,),
        out_shape=jax.ShapeDtypeStruct((2 * orbs, 2 * orbs), F32),
        in_specs=[spec, spec, spec],
        out_specs=pl.BlockSpec((2 * orbs, 2 * orbs), lambda x: (0, 0)),
        compiler_params=pltpu.CompilerParams(vmem_limit_bytes=24 << 20),
        cost_estimate=pl.CostEstimate(flops=int(1e9), bytes_accessed=int(9.5e6), transcendentals=0),
        name="chip_products",
    )(psi, half, par)


def cross_kernel(psi_ref, par_ref, g_ref, gpar_ref, far_ref, o_ref, acc):
    @pl.when(pl.program_id(0) == 0)
    def _():
        acc[...] = jnp.zeros_like(acc)

    planes = psi_ref.shape[1]
    upper = upper_chip()
    first = upper * (planes - WINDOW)
    keep = (1 - upper).astype(F32).astype(BF16)
    skipped = CUT - (planes - WINDOW)
    group = 6
    for z in range(0, WINDOW, group):
        def wide(ref, offset, masked):
            parts = [ref[0, offset + z + i] for i in range(group)]
            if masked:
                parts = [p * keep if z + i < skipped else p for i, p in enumerate(parts)]
            return jnp.concatenate(parts, axis=1)

        left = jnp.concatenate(
            [
                wide(psi_ref, first, True),
                wide(par_ref, first, True),
                wide(g_ref, 0, False),
                wide(gpar_ref, 0, False),
            ],
            axis=0,
        )
        acc[...] += contract(left, wide(far_ref, 0, False))

    @pl.when(pl.program_id(0) == pl.num_programs(0) - 1)
    def _():
        rows = acc.shape[0] // 2
        o_ref[...] = jnp.concatenate([acc[:rows], acc[rows:]], axis=1)


def cross_products(psi, par, g, g_par, far):
    layers, planes, orbs, ny = psi.shape
    whole = pl.BlockSpec((1, planes, orbs, ny), lambda x: (x, 0, 0, 0))
    part = pl.BlockSpec((1, WINDOW, orbs, ny), lambda x: (x, 0, 0, 0))
    return pl.pallas_call(
        cross_kernel,
        grid=(layers,),
        out_shape=jax.ShapeDtypeStruct((2 * orbs, 2 * orbs), F32),
        in_specs=[whole, whole, part, part, part],
        out_specs=pl.BlockSpec((2 * orbs, 2 * orbs), lambda x: (0, 0)),
        scratch_shapes=[pltpu.VMEM((4 * orbs, orbs), F32)],
        compiler_params=pltpu.CompilerParams(vmem_limit_bytes=24 << 20),
        cost_estimate=pl.CostEstimate(flops=int(1e9), bytes_accessed=int(11e6), transcendentals=0),
        name="cross_products",
    )(psi, par, g, g_par, far)


def gradient_kernel(cells, hpsi_ref, psi_ref, v_ref, sums_ref, o_ref, ray):
    orbs = o_ref.shape[0]

    @pl.when((pl.program_id(0) == 0) & (pl.program_id(1) == 0))
    def _():
        shape = (orbs, orbs)
        same = lax.broadcasted_iota(jnp.int32, shape, 0) == lax.broadcasted_iota(jnp.int32, shape, 1)

        def diagonal(rows):
            picked = jnp.where(same, sums_ref[rows : rows + orbs, :orbs], 0.0)
            return jnp.sum(picked, axis=1, keepdims=True) / cells

        ray[...] = jnp.broadcast_to(diagonal(orbs) / (diagonal(0) + 1e-06), ray.shape)

    rayleigh = ray[...]
    v = v_ref[0]
    parts = []
    for z in range(hpsi_ref.shape[1]):
        parts.append(
            (hpsi_ref[0, z] - rayleigh * psi_ref[0, z].astype(F32)) / (2.0 + v[z : z + 1])
        )
    o_ref[:, 0] = jnp.swapaxes(jnp.stack(parts, axis=0), 0, 1)


def gradient_of(hpsi, psi, potential, sums, cells):
    layers, planes, orbs, ny = psi.shape
    block = 8
    spec = pl.BlockSpec((1, block, orbs, ny), lambda x, z: (x, z, 0, 0))
    return pl.pallas_call(
        lambda *refs: gradient_kernel(cells, *refs),
        grid=(layers, planes // block),
        out_shape=jax.ShapeDtypeStruct((orbs, layers, planes, ny), F32),
        in_specs=[
            spec,
            spec,
            pl.BlockSpec((1, block, ny), lambda x, z: (x, z, 0)),
            pl.BlockSpec(sums.shape, lambda x, z: (0, 0)),
        ],
        out_specs=pl.BlockSpec((orbs, 1, block, ny), lambda x, z: (0, x, z, 0)),
        scratch_shapes=[pltpu.VMEM((orbs, ny), F32)],
        compiler_params=pltpu.CompilerParams(vmem_limit_bytes=16 << 20),
        cost_estimate=pl.CostEstimate(flops=int(1e7), bytes_accessed=int(16e6), transcendentals=0),
        name="gradient",
    )(hpsi, psi, potential, sums)


def body(orbitals, potential):
    orbs, layers, planes, ny = orbitals.shape
    grids = lax.axis_size("grid")
    cells = layers * grids * planes * ny
    band = lax.axis_index("band")
    upper, core = lax.div(band, 2), lax.rem(band, 2)
    other_core = [(0, 1), (1, 0), (2, 3), (3, 2)]
    other_chip = [(0, 2), (1, 3), (2, 0), (3, 1)]

    psi = jnp.transpose(orbitals, (1, 2, 0, 3))
    wanted = lax.dynamic_slice_in_dim(psi, (1 - upper) * (planes - WINDOW), WINDOW, 1)
    far = lax.ppermute(wanted, "band", other_chip)
    lo = lax.ppermute(psi[layers - REACH :], "grid", [(i, (i + 1) % grids) for i in range(grids)])
    hi = lax.ppermute(psi[:REACH], "grid", [((i + 1) % grids, i) for i in range(grids)])
    par = lax.ppermute(psi, "band", other_core)

    hpsi, half, g = stencil(psi, lo, hi, potential)
    g_par = lax.ppermute(g, "band", other_core)
    chip = grid_sum(chip_products(psi, half, par), 1)
    gradient = gradient_of(hpsi, psi, potential, chip, cells)

    cross = grid_sum(cross_products(psi, par, g, g_par, far), 2)
    cross_par = lax.ppermute(cross[orbs:], "band", other_core)
    cross_far = lax.ppermute(cross, "band", other_chip)

    def rows_of(which):
        mine = chip[which * orbs : (which + 1) * orbs]
        columns = slice(which * orbs, (which + 1) * orbs)
        turned = cross_far[:, columns].T
        own = cross[:orbs, columns] + turned[:, :orbs]
        par_columns = cross_par[:, columns] + turned[:, orbs:]
        first, second = mine[:, :orbs], mine[:, orbs:]
        near = jnp.where(core == 0, jnp.concatenate([first, second], 1), jnp.concatenate([second, first], 1))
        away = jnp.where(
            core == 0, jnp.concatenate([own, par_columns], 1), jnp.concatenate([par_columns, own], 1)
        )
        rows = jnp.where(upper == 0, jnp.concatenate([near, away], 1), jnp.concatenate([away, near], 1))
        return rows / cells

    return (gradient, rows_of(0), rows_of(1))


def solution(mesh):
    in_specs = (P("band", "grid", None, None), P("grid", None, None))
    out_specs = (P("band", "grid", None, None), P("band", None), P("band", None))
    return jax.shard_map(body, mesh=mesh, in_specs=in_specs, out_specs=out_specs, check_vma=False)
```

```python
import jax
import jax.numpy as jnp
from jax import lax
from jax.experimental import pallas as pl
from jax.experimental.pallas import tpu as pltpu
from jax.sharding import PartitionSpec as P

COEFFS = (-49.0 / 18.0, 3.0 / 2.0, -3.0 / 20.0, 1.0 / 90.0)
HALVED = tuple(-0.5 * c for c in COEFFS)
REACH = len(COEFFS) - 1
MESH = pl.DeviceIdType.MESH
F32 = jnp.float32
BF16 = jnp.bfloat16

CUT = 18
WINDOW = 18
EARLY = (4, 3)
FIRST = sum(EARLY)
SMALL = pl.CostEstimate(flops=1000, bytes_accessed=1000, transcendentals=0)


def upper_chip():
    return lax.div(lax.axis_index("band"), 2)


STRIDES = (1, 16, 4)
SIDE = 4


def sum_kernel(cells, near_ref, cross_ref, s_ref, h_ref, chip_ref, b0, bx, by, bz, qx, gy, gx, far, par, send_sem, recv_sem):
    me, band = lax.axis_index("grid"), lax.axis_index("band")
    upper, core = lax.div(band, 2), lax.rem(band, 2)
    rows = near_ref.shape[0]
    rows_x, rows_y = rows // SIDE, rows // SIDE // SIDE
    coord = [lax.rem(lax.div(me, s), SIDE) for s in STRIDES]
    far_band = lax.rem(band + 2, 4)
    par_band = band + 1 - 2 * core

    def peer(axis, d, of=band):
        other = lax.rem(coord[axis] + d, SIDE)
        return other, (of, me + (other - coord[axis]) * STRIDES[axis])

    barrier = pltpu.get_barrier_semaphore()

    def greet(device):
        pl.semaphore_signal(barrier, inc=1, device_id=device, device_id_type=MESH)

    for axis in range(3):
        for d in range(1, SIDE):
            greet(peer(axis, d)[1])
    for of in (far_band, par_band):
        for d in range(SIDE):
            greet(peer(0, d, of)[1])

    def send(phase, d, src, dst, device):
        copy = pltpu.make_async_remote_copy(
            src_ref=src,
            dst_ref=dst,
            send_sem=send_sem.at[phase, d],
            recv_sem=recv_sem.at[phase, d],
            device_id=device,
            device_id_type=MESH,
        )
        copy.start()
        return copy

    def exchange(phase, axis, source, landing):
        copies = []
        for d in range(1, SIDE):
            other, device = peer(axis, d)
            copies.append(send(phase, d, source(other), landing, device))
        return copies

    def finish(copies):
        for copy in copies:
            copy.wait()

    def total(ref):
        return (ref[0] + ref[1]) + (ref[2] + ref[3])

    x, y, z = coord
    for c in range(SIDE):
        b0[c, 0] = near_ref[c * rows_x : (c + 1) * rows_x]
        b0[c, 1] = cross_ref[c * rows_x : (c + 1) * rows_x]
    pl.semaphore_wait(barrier, 3 * (SIDE - 1) + 2 * SIDE)

    copies = exchange(0, 0, lambda c: b0.at[c], bx.at[x])
    bx[x] = b0[x]
    finish(copies)
    summed = total(bx)
    for c in range(SIDE):
        qx[c] = summed[:, c * rows_y : (c + 1) * rows_y]

    copies = exchange(1, 1, lambda c: qx.at[c], by.at[y])
    by[y] = qx[y]
    finish(copies)
    bz[z] = total(by)

    finish(exchange(2, 2, lambda c: bz.at[z], bz.at[z]))
    gy[y] = total(bz)

    finish(exchange(3, 1, lambda c: gy.at[y], gy.at[y]))
    for c in range(SIDE):
        gx[x, :, c * rows_y : (c + 1) * rows_y] = gy[c]

    copies = exchange(4, 0, lambda c: gx.at[x], gx.at[x])
    for d in range(SIDE):
        copies.append(send(5, d, gx.at[x, 1], far.at[x], peer(0, d, far_band)[1]))
        copies.append(send(6, d, gx.at[x, 1], par.at[x], peer(0, d, par_band)[1]))
    finish(copies)

    def whole(ref, i=None):
        return jnp.concatenate([ref[c] if i is None else ref[c, i] for c in range(SIDE)], axis=0)

    chip, cross = whole(gx, 0), whole(gx, 1)
    chip_ref[...] = chip
    orbs = rows // 2
    par_rows = jnp.concatenate([par[c] for c in range(SIDE // 2, SIDE)], axis=0)
    turned = whole(far).T
    for which, o_ref in ((0, s_ref), (1, h_ref)):
        columns = slice(which * orbs, (which + 1) * orbs)
        mine = chip[which * orbs : (which + 1) * orbs]
        away = turned[columns] + jnp.concatenate([cross[:orbs, columns], par_rows[:, columns]], axis=1)
        mine = jnp.where(core == 0, mine, pltpu.roll(mine, orbs, 1)) / cells
        away = jnp.where(core == 0, away, pltpu.roll(away, orbs, 1)) / cells
        o_ref[:, :rows] = jnp.where(upper == 0, mine, away)
        o_ref[:, rows:] = jnp.where(upper == 0, away, mine)


def sums_of(near, cross, cells, collective_id):
    rows, cols = near.shape
    rows_x, rows_y = rows // SIDE, rows // SIDE // SIDE
    vmem = pl.BlockSpec(memory_space=pltpu.VMEM)
    wide = pltpu.VMEM((SIDE, 2, rows_x, cols), F32)
    slim = pltpu.VMEM((SIDE, 2, rows_y, cols), F32)
    part = pltpu.VMEM((SIDE, rows_x, cols), F32)
    out = jax.ShapeDtypeStruct((rows // 2, 2 * rows), F32)
    return pl.pallas_call(
        lambda *refs: sum_kernel(cells, *refs),
        out_shape=(out, out, jax.ShapeDtypeStruct((rows, cols), F32)),
        in_specs=[vmem, vmem],
        out_specs=(vmem, vmem, vmem),
        scratch_shapes=[wide, wide, slim, slim, slim, slim, wide, part, part]
        + [pltpu.SemaphoreType.DMA((7, SIDE))] * 2,
        compiler_params=pltpu.CompilerParams(
            collective_id=collective_id, has_side_effects=True, vmem_limit_bytes=6 << 20
        ),
        name="grid_sums",
    )(near, cross)


def halo_kernel(psi_ref, lo_ref, hi_ref, far_ref, up_a, up_b, down_a, down_b, send_sem, recv_sem):
    me, band = lax.axis_index("grid"), lax.axis_index("band")
    x, row = lax.rem(me, SIDE), lax.div(me, SIDE)
    rows = SIDE * SIDE
    after, before = lax.rem(row + 1, rows), lax.rem(row + rows - 1, rows)
    layers, planes = psi_ref.shape[:2]
    share = planes // SIDE
    last = SIDE - 1

    def device(column, line):
        return (band, line * SIDE + column)

    barrier = pltpu.get_barrier_semaphore()
    for d in range(1, SIDE):
        pl.semaphore_signal(
            barrier, inc=1, device_id=device(lax.rem(x + d, SIDE), row), device_id_type=MESH
        )
    for line in (after, before):
        pl.semaphore_signal(barrier, inc=1, device_id=device(x, line), device_id_type=MESH)
    twin = (lax.rem(band + 2, 4), me)
    pl.semaphore_signal(barrier, inc=1, device_id=twin, device_id_type=MESH)
    pl.semaphore_wait(barrier, SIDE + 2)

    tail = psi_ref.at[pl.ds(layers - REACH, REACH)]
    head = psi_ref.at[pl.ds(0, REACH)]

    def piece(ref, q):
        start = q * share
        return ref.at[:, pl.ds(start if isinstance(q, int) else pl.multiple_of(start, share), share)]

    def copy(src, dst, sent, received, target):
        return pltpu.make_async_remote_copy(
            src_ref=src,
            dst_ref=dst,
            send_sem=send_sem.at[sent],
            recv_sem=recv_sem.at[received],
            device_id=target,
            device_id_type=MESH,
        )

    LO, HI, UP_A, UP_B, DOWN_A, DOWN_B, LO_PART, HI_PART = 0, 1, 2, 3, 4, 5, 6, 6 + SIDE
    FAR = 6 + 2 * SIDE
    own = device(x, row)
    wanted = (1 - upper_chip()) * (planes - WINDOW)

    def far_copy(i):
        begin = sum(EARLY[:i])
        return copy(
            psi_ref.at[:, pl.ds(wanted + begin, EARLY[i])],
            far_ref.at[:, pl.ds(begin, EARLY[i])],
            10 + i,
            FAR + i,
            twin,
        )

    @pl.when(x == last)
    def _():
        for q in range(last):
            copy(piece(tail, q), up_a, q, UP_A, device(q, row)).start()
        copy(piece(tail, last), up_b, 6, UP_B, device(x, after)).start()

    @pl.when(x == 0)
    def _():
        for q in range(1, SIDE):
            copy(piece(head, q), down_a, q, DOWN_A, device(q, row)).start()
        copy(piece(head, 0), down_b, 7, DOWN_B, device(x, before)).start()

    @pl.when(x < last)
    def _():
        copy(tail, lo_ref, 4, LO, device(x + 1, row)).start()

    @pl.when(x > 0)
    def _():
        copy(head, hi_ref, 5, HI, device(x - 1, row)).start()

    far_copy(0).start()

    @pl.when(x < last)
    def _():
        copy(piece(tail, 0), up_a, 0, UP_A, own).wait_recv()

    @pl.when(x == 0)
    def _():
        copy(up_a, piece(lo_ref, 0), 6, LO_PART, device(x, after)).start()

    @pl.when((x > 0) & (x < last))
    def _():
        copy(up_a, up_b, 6, UP_B, device(x, after)).start()

    @pl.when(x > 0)
    def _():
        copy(piece(head, 0), down_a, 0, DOWN_A, own).wait_recv()

    @pl.when(x == last)
    def _():
        copy(down_a, piece(hi_ref, last), 7, HI_PART + last, device(x, before)).start()

    @pl.when((x > 0) & (x < last))
    def _():
        copy(down_a, down_b, 7, DOWN_B, device(x, before)).start()

    far_copy(1).start()

    @pl.when(x > 0)
    def _():
        copy(up_a, up_b, 6, UP_B, own).wait_recv()
        copy(up_b, piece(lo_ref, x), 8, LO_PART + x, device(0, row)).start()

    @pl.when(x < last)
    def _():
        copy(down_a, down_b, 7, DOWN_B, own).wait_recv()
        copy(down_b, piece(hi_ref, x), 9, HI_PART + x, device(last, row)).start()

    @pl.when(x == 0)
    def _():
        for q in range(SIDE):
            copy(up_b, piece(lo_ref, q), 8, LO_PART + q, own).wait_recv()
        for q in range(1, SIDE):
            copy(piece(head, q), down_a, q, DOWN_A, own).wait_send()

    @pl.when(x == last)
    def _():
        for q in range(SIDE):
            copy(down_b, piece(hi_ref, q), 9, HI_PART + q, own).wait_recv()
        for q in range(last):
            copy(piece(tail, q), up_a, q, UP_A, own).wait_send()

    @pl.when(x > 0)
    def _():
        copy(tail, lo_ref, 4, LO, own).wait_recv()
        copy(head, hi_ref, 5, HI, own).wait_send()
        copy(up_b, piece(lo_ref, 0), 8, LO_PART, own).wait_send()

    @pl.when(x < last)
    def _():
        copy(head, hi_ref, 5, HI, own).wait_recv()
        copy(tail, lo_ref, 4, LO, own).wait_send()
        copy(down_b, piece(hi_ref, 0), 9, HI_PART, own).wait_send()

    copy(up_a, up_b, 6, UP_B, own).wait_send()
    copy(down_a, down_b, 7, DOWN_B, own).wait_send()
    for i in range(len(EARLY)):
        far_copy(i).wait()


def halo(psi, collective_id):
    layers, planes, orbs, ny = psi.shape
    edge = jax.ShapeDtypeStruct((REACH, planes, orbs, ny), psi.dtype)
    part = pltpu.VMEM((REACH, planes // SIDE, orbs, ny), psi.dtype)
    return pl.pallas_call(
        halo_kernel,
        out_shape=(edge, edge, jax.ShapeDtypeStruct((layers, FIRST, orbs, ny), psi.dtype)),
        in_specs=[pl.BlockSpec(memory_space=pl.ANY)],
        out_specs=(pl.BlockSpec(memory_space=pl.ANY),) * 3,
        scratch_shapes=[
            part,
            part,
            part,
            part,
            pltpu.SemaphoreType.DMA((12,)),
            pltpu.SemaphoreType.DMA((8 + 2 * SIDE,)),
        ],
        compiler_params=pltpu.CompilerParams(
            collective_id=collective_id, has_side_effects=True, vmem_limit_bytes=8 << 20
        ),
        cost_estimate=SMALL,
        name="halo",
    )(psi)


def stencil_kernel(psi_ref, lo_ref, hi_ref, v_ref, hpsi_ref, half_ref, g_ref, field):
    layers, planes = psi_ref.shape[:2]

    @pl.when(pl.program_id(0) == 0)
    def _():
        edge = jnp.zeros((layers + 2 * REACH, REACH) + psi_ref.shape[2:], F32)
        field[:, :REACH] = edge
        field[:, REACH + planes :] = edge

    @pl.loop(0, planes, unroll=4)
    def _(z):
        for x in range(REACH):
            field[x, z + REACH] = lo_ref[x, z].astype(F32)
            field[x + REACH + layers, z + REACH] = hi_ref[x, z].astype(F32)
        for x in range(layers):
            field[x + REACH, z + REACH] = psi_ref[x, z].astype(F32)

    @pl.loop(0, planes, unroll=4)
    def _(z):
        for x in range(layers):
            i, j = x + REACH, z + REACH
            center = field[i, j]
            total = (3.0 * HALVED[0] + v_ref[x, pl.ds(z, 1), :]) * center
            for k in range(1, REACH + 1):
                pair_x = field[i + k, j] + field[i - k, j]
                pair_z = field[i, j + k] + field[i, j - k]
                pair_y = pltpu.roll(center, k, 1) + pltpu.roll(center, center.shape[1] - k, 1)
                total = total + HALVED[k] * (pair_x + pair_z + pair_y)
            hpsi_ref[x, z] = total
            half_ref[x, z] = total.astype(BF16)

    upper = upper_chip()
    first = upper * (planes - WINDOW)

    @pl.loop(0, WINDOW, unroll=2)
    def _(i):
        for x in range(layers):
            g_ref[x, i] = half_ref[x, first + i]

    @pl.when(upper == 1)
    def _():
        for x in range(layers):
            for z in range(planes - WINDOW, CUT + REACH):
                if z < CUT:
                    total = jnp.zeros(psi_ref.shape[2:], F32)
                    for k in range(CUT - z, REACH + 1):
                        total = total + HALVED[k] * field[x + REACH, z + REACH + k]
                else:
                    total = hpsi_ref[x, z]
                    for k in range(z - CUT + 1, REACH + 1):
                        total = total - HALVED[k] * field[x + REACH, z + REACH - k]
                g_ref[x, z - (planes - WINDOW)] = total.astype(BF16)


def stencil(psi, lo, hi, potential):
    layers, planes, orbs, ny = psi.shape
    block = 16

    def spec(n, m):
        return pl.BlockSpec((n, m, block, ny), lambda o: (0, 0, o, 0))

    return pl.pallas_call(
        stencil_kernel,
        grid=(orbs // block,),
        out_shape=(
            jax.ShapeDtypeStruct(psi.shape, F32),
            jax.ShapeDtypeStruct(psi.shape, BF16),
            jax.ShapeDtypeStruct((layers, WINDOW, orbs, ny), BF16),
        ),
        in_specs=[
            spec(layers, planes),
            spec(REACH, planes),
            spec(REACH, planes),
            pl.BlockSpec(potential.shape, lambda o: (0, 0, 0)),
        ],
        out_specs=(spec(layers, planes), spec(layers, planes), spec(layers, WINDOW)),
        scratch_shapes=[pltpu.VMEM((layers + 2 * REACH, planes + 2 * REACH, block, ny), F32)],
        compiler_params=pltpu.CompilerParams(vmem_limit_bytes=40 << 20),
        cost_estimate=SMALL,
        name="stencil",
    )(psi, lo, hi, potential)


def partner_kernel(src_ref, dst_ref, send_sem, recv_sem):
    band, me = lax.axis_index("band"), lax.axis_index("grid")
    partner = (band + 1 - 2 * lax.rem(band, 2), me)
    barrier = pltpu.get_barrier_semaphore()
    pl.semaphore_signal(barrier, inc=1, device_id=partner, device_id_type=MESH)
    pl.semaphore_wait(barrier, 1)
    copy = pltpu.make_async_remote_copy(
        src_ref=src_ref,
        dst_ref=dst_ref,
        send_sem=send_sem,
        recv_sem=recv_sem,
        device_id=partner,
        device_id_type=MESH,
    )
    copy.start()
    copy.wait()


def from_partner(array, collective_id):
    return pl.pallas_call(
        partner_kernel,
        out_shape=jax.ShapeDtypeStruct(array.shape, array.dtype),
        in_specs=[pl.BlockSpec(memory_space=pl.ANY)],
        out_specs=pl.BlockSpec(memory_space=pl.ANY),
        scratch_shapes=[pltpu.SemaphoreType.DMA, pltpu.SemaphoreType.DMA],
        compiler_params=pltpu.CompilerParams(
            collective_id=collective_id, has_side_effects=True, vmem_limit_bytes=1 << 20
        ),
        cost_estimate=SMALL,
        name="from_partner",
    )(array)


def contract(left, right):
    return lax.dot_general(left, right, (((1,), (1,)), ((), ())), preferred_element_type=F32)


def chip_kernel(psi_ref, half_ref, par_ref, o_ref):
    @pl.when(pl.program_id(0) == 0)
    def _():
        o_ref[...] = jnp.zeros_like(o_ref)

    planes = psi_ref.shape[1]
    group = 8
    for z in range(0, planes, group):
        def wide(ref):
            return jnp.concatenate([ref[0, z + i] for i in range(group)], axis=1)

        psi = wide(psi_ref)
        left = jnp.concatenate([psi, wide(half_ref)], axis=0)
        right = jnp.concatenate([psi, wide(par_ref)], axis=0)
        o_ref[...] += contract(left, right)


def chip_products(psi, half, par):
    layers, planes, orbs, ny = psi.shape
    spec = pl.BlockSpec((1, planes, orbs, ny), lambda x: (x, 0, 0, 0))
    return pl.pallas_call(
        chip_kernel,
        grid=(layers,),
        out_shape=jax.ShapeDtypeStruct((2 * orbs, 2 * orbs), F32),
        in_specs=[spec, spec, spec],
        out_specs=pl.BlockSpec((2 * orbs, 2 * orbs), lambda x: (0, 0)),
        compiler_params=pltpu.CompilerParams(vmem_limit_bytes=24 << 20),
        cost_estimate=SMALL,
        name="chip_products",
    )(psi, half, par)


def cross_kernel(begin, psi_ref, par_ref, g_ref, gpar_ref, far_ref, *rest):
    acc = rest[-1]

    @pl.when(pl.program_id(0) == 0)
    def _():
        acc[...] = jnp.zeros_like(acc) if begin == 0 else rest[0][...]

    planes, count = psi_ref.shape[1], far_ref.shape[1]
    upper = upper_chip()
    first = upper * (planes - WINDOW)
    keep = (1 - upper).astype(F32).astype(BF16)
    skipped = CUT - (planes - WINDOW)
    group = 4
    for z in range(0, count, group):
        mine = range(z, min(z + group, count))

        def wide(ref, offset, masked=False):
            parts = [ref[0, offset + i] for i in mine]
            if masked:
                parts = [p * keep if begin + i < skipped else p for i, p in zip(mine, parts)]
            return jnp.concatenate(parts, axis=1)

        left = jnp.concatenate(
            [
                wide(psi_ref, first + begin, True),
                wide(par_ref, first + begin, True),
                wide(g_ref, begin),
                wide(gpar_ref, begin),
            ],
            axis=0,
        )
        acc[...] += contract(left, wide(far_ref, 0))

    if begin:
        o_ref = rest[1]

        @pl.when(pl.program_id(0) == pl.num_programs(0) - 1)
        def _():
            rows = acc.shape[0] // 2
            o_ref[...] = jnp.concatenate([acc[:rows], acc[rows:]], axis=1)


def cross_products(psi, par, g, g_par, far, begun=None):
    layers, planes, orbs, ny = psi.shape
    begin = 0 if begun is None else FIRST

    def spec(n):
        return pl.BlockSpec((1, n, orbs, ny), lambda x: (x, 0, 0, 0))

    def fixed(shape):
        return pl.BlockSpec(shape, lambda x: (0, 0))

    tall, square = (4 * orbs, orbs), (2 * orbs, 2 * orbs)
    shape = square if begin else tall
    return pl.pallas_call(
        lambda *refs: cross_kernel(begin, *refs),
        grid=(layers,),
        out_shape=jax.ShapeDtypeStruct(shape, F32),
        in_specs=[spec(planes), spec(planes), spec(WINDOW), spec(WINDOW), spec(far.shape[1])]
        + ([fixed(tall)] if begin else []),
        out_specs=fixed(shape),
        scratch_shapes=[pltpu.VMEM(tall, F32)] if begin else [],
        compiler_params=pltpu.CompilerParams(vmem_limit_bytes=24 << 20),
        cost_estimate=SMALL,
        name="cross_products_%d" % begin,
    )(psi, par, g, g_par, far, *([begun] if begin else []))


def turn_kernel(hpsi_ref, v_ref, o_ref):
    v = v_ref[0]
    parts = [hpsi_ref[0, z] / (2.0 + v[z : z + 1]) for z in range(hpsi_ref.shape[1])]
    o_ref[:, 0] = jnp.swapaxes(jnp.stack(parts, axis=0), 0, 1)


def turn(hpsi, potential):
    layers, planes, orbs, ny = hpsi.shape
    block = 8
    return pl.pallas_call(
        turn_kernel,
        grid=(layers, planes // block),
        out_shape=jax.ShapeDtypeStruct((orbs, layers, planes, ny), F32),
        in_specs=[
            pl.BlockSpec((1, block, orbs, ny), lambda x, z: (x, z, 0, 0)),
            pl.BlockSpec((1, block, ny), lambda x, z: (x, z, 0)),
        ],
        out_specs=pl.BlockSpec((orbs, 1, block, ny), lambda x, z: (0, x, z, 0)),
        compiler_params=pltpu.CompilerParams(vmem_limit_bytes=16 << 20),
        cost_estimate=SMALL,
        name="turn",
    )(hpsi, potential)


def gradient_kernel(cells, part_ref, psi_ref, v_ref, sums_ref, o_ref, ray, weight):
    orbs = ray.shape[0]
    block = o_ref.shape[0]

    @pl.when(pl.program_id(0) == 0)
    def _():
        shape = (orbs, orbs)
        same = lax.broadcasted_iota(jnp.int32, shape, 0) == lax.broadcasted_iota(jnp.int32, shape, 1)

        def diagonal(rows):
            picked = jnp.where(same, sums_ref[rows : rows + orbs, :orbs], 0.0)
            return jnp.sum(picked, axis=1, keepdims=True) / cells

        ray[...] = jnp.broadcast_to(diagonal(orbs) / (diagonal(0) + 1e-06), ray.shape)
        weight[...] = 1.0 / (2.0 + v_ref[...])

    for i in range(block):
        rayleigh = ray[pl.ds(pl.program_id(0) * block + i, 1), :]
        for x in range(o_ref.shape[1]):
            o_ref[i, x] = part_ref[i, x] - (rayleigh * weight[x]) * psi_ref[i, x].astype(F32)


def gradient_of(part, orbitals, potential, sums, cells):
    orbs, layers, planes, ny = orbitals.shape
    block = 8
    spec = pl.BlockSpec((block, layers, planes, ny), lambda o: (o, 0, 0, 0))
    return pl.pallas_call(
        lambda *refs: gradient_kernel(cells, *refs),
        grid=(orbs // block,),
        out_shape=jax.ShapeDtypeStruct(orbitals.shape, F32),
        in_specs=[
            spec,
            spec,
            pl.BlockSpec(potential.shape, lambda o: (0, 0, 0)),
            pl.BlockSpec(sums.shape, lambda o: (0, 0)),
        ],
        out_specs=spec,
        scratch_shapes=[pltpu.VMEM((orbs, ny), F32), pltpu.VMEM(potential.shape, F32)],
        compiler_params=pltpu.CompilerParams(vmem_limit_bytes=16 << 20),
        name="gradient",
    )(part, orbitals, potential, sums)


def body(orbitals, potential):
    orbs, layers, planes, ny = orbitals.shape
    cells = layers * lax.axis_size("grid") * planes * ny
    upper = upper_chip()
    other_core = [(0, 1), (1, 0), (2, 3), (3, 2)]
    other_chip = [(0, 2), (1, 3), (2, 0), (3, 1)]

    psi = jnp.transpose(orbitals, (1, 2, 0, 3))
    par = lax.ppermute(psi, "band", other_core)
    lo, hi, far_first = halo(psi, 3)
    begin = (1 - upper) * (planes - WINDOW) + FIRST
    wanted = lax.dynamic_slice_in_dim(psi, begin, WINDOW - FIRST, 1)
    wanted, far_first, lo = lax.optimization_barrier((wanted, far_first, lo))
    far = lax.ppermute(wanted, "band", other_chip)

    hpsi, half, g = stencil(psi, lo, hi, potential)
    g_par = from_partner(g, 2)
    near = chip_products(psi, half, par)
    part = turn(hpsi, potential)
    begun = cross_products(psi, par, g, g_par, far_first)
    far, part, near, begun = lax.optimization_barrier((far, part, near, begun))
    cross = cross_products(psi, par, g, g_par, far, begun)
    intersection, subspace, chip = sums_of(near, cross, cells, 1)
    gradient = gradient_of(part, orbitals, potential, chip, cells)
    return (gradient, intersection, subspace)


def solution(mesh):
    in_specs = (P("band", "grid", None, None), P("grid", None, None))
    out_specs = (P("band", "grid", None, None), P("band", None), P("band", None))
    return jax.shard_map(body, mesh=mesh, in_specs=in_specs, out_specs=out_specs, check_vma=False)
```
